256 devices in a mesh: dp: 16 (over y, x_lo, core), vocab: 16 (over x_hi, z).
Axes of the slice: x: 4 (x_hi: 2, x_lo: 2; x = x_hi * 2 + x_lo), y: 4, z: 8, core: 2. Of those that a mesh axis runs over, the one named last changes fastest.
Arguments:
- hidden: bfloat16 [2048, 12288], P('dp'), may hold values from -8 to 8
- head_weight: bfloat16 [12288, 32768], P('dp', 'vocab'), may hold values from -0.16237976 to 0.16237976
- targets: int32 [2048], replicated, may hold values from 0 to 32767
Outputs:
- loss: float32 [2048], P('dp')
- grad_weight: float32 [12288, 32768], P('dp', 'vocab')
The draws below stay inside these ranges and needn't reach their ends.
All inputs are finite; a program needn't handle non-finite values.
Results may differ from the reference program's by a relative error of at most 0.0014.
Values may be sent and summed in bfloat16 or wider, within the bound.
No kernel may reach another device: no remote copies, remote signals or barrier semaphores. Data moves between devices by JAX's collectives and lax.ppermute only.
A program may use at most 128 MiB of HBM per device.

```python
import math
import jax
import jax.numpy as jnp
from jax import lax

D = 12288
V = 32768
TOKEN_COUNT = 2048


def weight_column(key, index):
    base = jax.random.fold_in(jax.random.fold_in(key, 7151), index)
    column = jax.random.normal(base, (D,), jnp.float32)
    return jnp.clip(column, -6.0, 6.0) * (3.0 / math.sqrt(D))


def draw_head_weight(key, part):
    columns = jax.vmap(lambda index: weight_column(key, index))(jnp.arange(V, dtype=jnp.int32))
    return columns.T.astype(jnp.bfloat16)


def draw_hidden(key, part):
    values = jax.random.normal(jax.random.fold_in(key, 313), (TOKEN_COUNT, D), jnp.float32)
    return jnp.clip(values, -8.0, 8.0).astype(jnp.bfloat16)


def touch_ends(result, key, least, largest):
    place = [jax.random.randint(jax.random.fold_in(key, axis), (), 0, length) for axis, length in enumerate(result.shape)]
    longest = result.shape.index(max(result.shape))
    next_to = place[:longest] + [(place[longest] + 1) % result.shape[longest]] + place[longest + 1:]
    return result.at[tuple(place)].set(least).at[tuple(next_to)].set(largest)


def setup_inputs(seed: int = 0) -> dict:
    keys = jax.random.split(jax.random.key(seed), 4)
    return {
        "hidden": draw_hidden(jax.random.fold_in(keys[3], 71), 0),
        "head_weight": draw_head_weight(jax.random.fold_in(keys[3], 71), 0),
        "targets": touch_ends(jax.random.randint(keys[2], (TOKEN_COUNT,), 0, V), jax.random.fold_in(keys[2], 1), 0, V - 1).astype(jnp.int32),
    }


def reference(hidden, head_weight, targets):
    logits = jnp.dot(hidden, head_weight, preferred_element_type=jnp.float32)
    peak = jnp.max(logits, axis=1)
    total = jnp.sum(jnp.exp(logits - peak[:, None]), axis=1)
    columns = jnp.arange(logits.shape[1], dtype=jnp.int32)
    onehot = targets[:, None] == columns[None, :]
    picked = jnp.sum(jnp.where(onehot, logits, 0.0), axis=1)
    spread = peak + jnp.log(total)
    loss = spread - picked
    slope = (jnp.exp(logits - spread[:, None]) - onehot.astype(jnp.float32)).astype(jnp.bfloat16)
    grad_weight = lax.dot_general(hidden, slope, (((0,), (0,)), ((), ())), preferred_element_type=jnp.float32)
    return loss, grad_weight
```

```python
import jax
import jax.numpy as jnp
from jax import lax
from jax.sharding import PartitionSpec as P


AXES = ("dp", "vocab")
Y, X, C = 4, 2, 2
LANES = 128


def place(y, x, c):
    return ((y % Y) * X + x) * C + c


def table(dy, dx, dc):
    return [
        (place(y + dy, x ^ dx, c ^ dc), place(y, x, c))
        for y in range(Y)
        for x in range(X)
        for c in range(C)
    ]


def outer_table(dy):
    out = []
    for y in range(Y):
        for x in range(X):
            for c in range(C):
                for h in range(2):
                    for z in range(8):
                        out.append(
                            (
                                place(y + dy, x ^ 1, c) * 16 + (h ^ 1) * 8 + z,
                                place(y, x, c) * 16 + h * 8 + z,
                            )
                        )
    return out


def fetch(value, dy, dx, dc=0):
    return lax.ppermute(value, "dp", table(dy, dx, dc))


def fetch_outer(value, dy):
    return lax.ppermute(value, AXES, outer_table(dy))


def encode(values):
    peak = jnp.max(jnp.abs(values), axis=-1, keepdims=True)
    power = jnp.ceil(jnp.log2(jnp.maximum(peak, 1e-30) * (1.0 / 32000.0)))
    codes = jnp.round(values * jnp.exp2(-power)).astype(jnp.int16)
    tail = jnp.broadcast_to(power.astype(jnp.int16), (*values.shape[:-1], LANES))
    return jnp.concatenate([codes, tail], axis=-1)


def decode(codes):
    width = codes.shape[-1] - LANES
    power = codes[..., width : width + 1].astype(jnp.float32)
    return codes[..., :width].astype(jnp.float32) * jnp.exp2(power)


def per_device(hidden, head_weight, targets):
    here = lax.axis_index("dp")
    block_index = lax.axis_index("vocab")
    c = here % C
    x = (here // C) % X
    y = here // (C * X)
    rows = hidden.shape[0]
    depth, width = head_weight.shape
    half = rows // 2

    partner_weight = fetch(head_weight, 0, 0, 1)
    weight = jnp.concatenate([head_weight, partner_weight], axis=0)

    parts = {}
    for dx in (1, 0):
        for dy in (2, 1, 3, 0):
            chip = ((y - dy) % Y) * X + (x ^ dx)
            own = lax.dynamic_slice_in_dim(hidden, (chip * C + c) * depth, depth, 1)
            other = lax.dynamic_slice_in_dim(hidden, (chip * C + 1 - c) * depth, depth, 1)
            piece = jnp.concatenate([own, other], axis=1)
            if dx == 1 and dy in (1, 3):
                piece = fetch_outer(piece, dy)
            elif (dx, dy) != (0, 0):
                piece = fetch(piece, dy, dx)
            parts[dy, dx] = piece

    def product(keys, a, b):
        left = jnp.concatenate([parts[k][a:b] for k in keys], axis=0)
        out = jnp.dot(left, weight, preferred_element_type=jnp.float32)
        return out.reshape(len(keys), b - a, width)

    sent = encode(product([(d, 1) for d in range(Y)], 0, half))
    kept = product([(d, 0) for d in range(Y)], 0, half)
    summed = kept + decode(fetch(sent, 0, 1))
    first = summed[0]
    pieces = [fetch(encode(summed[d]), -d, 0) for d in (2, 1, 3)]
    for piece in pieces:
        first = first + decode(piece)

    pieces = [fetch(encode(product([(d, 0), (d, 1)], half, rows)), -d, 0) for d in (2, 1, 3)]
    summed = product([(0, 0), (0, 1)], half, rows)
    for piece in pieces:
        summed = summed + decode(piece)
    second = summed[0] + decode(fetch(encode(summed[1]), 0, 1))

    labels = lax.dynamic_slice_in_dim(targets, here * rows, rows, 0)
    columns = block_index * width + jnp.arange(width, dtype=jnp.int32)

    def local(logits, label):
        onehot = label[:, None] == columns[None, :]
        peak = jnp.max(logits, axis=1)
        raised = jnp.exp(logits - peak[:, None])
        total = jnp.sum(raised, axis=1)
        picked = jnp.sum(jnp.where(onehot, logits, 0.0), axis=1)
        return raised.astype(jnp.bfloat16), peak, total, picked

    e1, m1, s1, p1 = local(first, labels[:half])
    e2, m2, s2, p2 = local(second, labels[half:])

    near1 = jnp.stack([e1] + [fetch(e1, d, 0) for d in (1, 2, 3)])
    near2 = jnp.stack([e2, fetch(e2, 0, 1)])
    far1 = fetch(near1, 0, 1)
    far2 = [near2] + [fetch(near2, d, 0) for d in (1, 2, 3)]

    peak = jnp.concatenate([m1, m2])
    stats = jnp.stack([peak, jnp.concatenate([s1, s2]), jnp.concatenate([p1, p2])])
    every = lax.all_to_all(
        jnp.broadcast_to(stats[None], (16, *stats.shape)), "vocab", 0, 0, tiled=True
    )
    top = jnp.max(every[:, 0], axis=0)
    total = jnp.sum(every[:, 1] * jnp.exp(every[:, 0] - top[None]), axis=0)
    loss = top + jnp.log(total) - jnp.sum(every[:, 2], axis=0)
    factor = jnp.exp(peak - top) / total
    factors = lax.all_to_all(
        jnp.broadcast_to(factor[None], (16, rows)), "dp", 0, 0, tiled=True
    )

    def order(values):
        return values

    near = jnp.stack([near1, far1], axis=1)
    far = jnp.stack(far2, axis=0)
    raised = jnp.concatenate([near, far], axis=2)
    owners = jnp.stack(
        [jnp.stack([((y + dy) % Y) * X + (x ^ dx) for dx in range(X)]) for dy in range(Y)]
    ).reshape(-1)
    own_rows = owners * C + c
    scale = factors[own_rows]
    label = targets.reshape(16, rows)[own_rows]
    slope = (
        raised.reshape(8, rows, width).astype(jnp.float32) * scale[:, :, None]
        - (label[:, :, None] == columns[None, None, :]).astype(jnp.float32)
    ).astype(jnp.bfloat16)
    slope = slope.reshape(8 * rows, width)
    slope_other = fetch(slope, 0, 0, 1)

    states = jnp.concatenate([parts[dy, dx] for dy in range(Y) for dx in range(X)], axis=0)
    mine = states[:, :depth]
    partners = fetch(states[:, depth:], 0, 0, 1)
    dims = (((0,), (0,)), ((), ()))
    grad = lax.dot_general(
        jnp.concatenate([mine, partners], axis=0),
        jnp.concatenate([slope, slope_other], axis=0),
        dims,
        preferred_element_type=jnp.float32,
    )
    return (loss, grad)


def solution(mesh):
    in_specs = (P("dp", None), P("dp", "vocab"), P())
    out_specs = (P("dp"), P("dp", "vocab"))
    return jax.shard_map(
        per_device, mesh=mesh, in_specs=in_specs, out_specs=out_specs, check_vma=False
    )
```

```python
import jax
import jax.numpy as jnp
from jax import lax
from jax.experimental import pallas as pl
from jax.experimental.pallas import tpu as pltpu
from jax.sharding import PartitionSpec as P


AXES = ("dp", "vocab")
Y, X, C, H, Z = 4, 2, 2, 2, 8
LANES = 128
ROWS_SUM = 48
ROWS_OUT = 80
F32, BF16 = jnp.float32, jnp.bfloat16


def device(y, x, c, h, z):
    return ((((y % Y) * X + x) * C + c) * H + h) * Z + z % Z


def fetch(value, source):
    pairs = [
        (device(*source(y, x, c, h, z)), device(y, x, c, h, z))
        for y in range(Y)
        for x in range(X)
        for c in range(C)
        for h in range(H)
        for z in range(Z)
    ]
    return lax.ppermute(value, AXES, pairs)


def from_y(value, dy):
    return fetch(value, lambda y, x, c, h, z: (y + dy, x, c, h, z))


def from_x(value):
    return fetch(value, lambda y, x, c, h, z: (y, x ^ 1, c, h, z))


def from_z(value, dz):
    return fetch(value, lambda y, x, c, h, z: (y, x, c, h, z + dz))


def from_core(value):
    return fetch(value, lambda y, x, c, h, z: (y, x, c ^ 1, h, z))


def side(dy, z):
    return (z + 1) % 2 if dy == 3 else z % 2


def encode(values):
    peak = jnp.max(jnp.abs(values), axis=-1, keepdims=True)
    power = jnp.ceil(jnp.log2(jnp.maximum(peak, 1e-30) * (1.0 / 32000.0)))
    codes = jnp.round(values * jnp.exp2(-power)).astype(jnp.int32).astype(jnp.int16)
    tail = jnp.broadcast_to(power, (values.shape[0], LANES)).astype(jnp.int32)
    return codes, tail.astype(jnp.int16)


def put(ref, index, values):
    width = values.shape[-1]
    codes, tail = encode(values)
    ref[(*index, slice(0, width))] = codes
    ref[(*index, slice(width, width + LANES))] = tail


def get(ref, index):
    width = ref.shape[-1] - LANES
    power = ref[(*index, slice(width, width + LANES))].astype(jnp.int32).astype(F32)
    codes = ref[(*index, slice(0, width))].astype(jnp.int32).astype(F32)
    return codes * jnp.exp2(power[:, :1])


def rows_of(refs, flag, dy, dx):
    near, far = refs[dy]
    far = jnp.concatenate([f[...] for f in far], axis=0)
    direct = flag == (dx if dy != 3 else 1 - dx)
    return jnp.where(direct, near[...], far)


def full(shape):
    return pl.BlockSpec(shape, lambda j: (0,) * len(shape))


STEPS = 4


def products(flag, near, far, extra, weights, sends):
    w0, w1 = weights
    depth, width = w0.shape
    block = width // STEPS
    a = ROWS_SUM
    rows = near[1].shape[0]
    b = rows - a
    groups = 3 if sends else 5
    flat = [near[1], near[2], near[3], *far[1], *far[2], *far[3], *extra]

    def body(flag_ref, *refs):
        refs = list(refs)
        n1, n2, n3, f1, f2a, f2b, f3 = refs[:7]
        rest = refs[7 : 7 + len(extra)]
        w0_ref, w1_ref = refs[7 + len(extra) : 9 + len(extra)]
        outs = refs[9 + len(extra) :]
        left, acc = outs[-2:]
        j = pl.program_id(0)
        by = {1: (n1, [f1]), 2: (n2, [f2a, f2b]), 3: (n3, [f3])}

        @pl.when(j == 0)
        def _():
            for k, dy in enumerate((1, 2, 3)):
                left[k * rows : (k + 1) * rows] = rows_of(by, flag_ref[0], dy, 1 if sends else 0)
            for k, ref in enumerate(rest):
                left[(3 + k) * rows : (4 + k) * rows] = ref[...]

        value = jnp.dot(left[:, :depth], w0_ref[...], preferred_element_type=F32)
        value += jnp.dot(left[:, depth:], w1_ref[...], preferred_element_type=F32)
        if not sends:
            outs[0][...] = value
            outs[1][...] = jnp.zeros((8, LANES), jnp.int32)
            return
        acc[j] = value

        @pl.when(j == STEPS - 1)
        def _():
            xs, ys = outs[0], outs[1:4]
            for k in range(3):
                whole = jnp.concatenate(
                    [acc[s, k * rows : (k + 1) * rows] for s in range(STEPS)], axis=1
                )
                put(xs, (k, slice(None)), whole[:a])
                put(ys[k], (slice(None),), whole[a:])

    if sends:
        shapes = [(3, a, width + LANES)] + [(b, width + LANES)] * 3
        out_shape = [jax.ShapeDtypeStruct(s, jnp.int16) for s in shapes]
        out_specs = [full(s) for s in shapes]
        acc_shape = (STEPS, groups * rows, block)
    else:
        out_shape = [
            jax.ShapeDtypeStruct((groups * rows, width), F32),
            jax.ShapeDtypeStruct((8, LANES), jnp.int32),
        ]
        out_specs = [
            pl.BlockSpec((groups * rows, block), lambda j: (0, j)),
            full((8, LANES)),
        ]
        acc_shape = (1, 8, LANES)
    return pl.pallas_call(
        body,
        grid=(STEPS,),
        in_specs=[pl.BlockSpec(memory_space=pltpu.SMEM)]
        + [full(v.shape) for v in flat]
        + [pl.BlockSpec((depth, block), lambda j: (0, j))] * 2,
        out_specs=out_specs,
        out_shape=out_shape,
        scratch_shapes=[
            pltpu.VMEM((groups * rows, 2 * depth), BF16),
            pltpu.VMEM(acc_shape, F32),
        ],
        name="sends" if sends else "keeps",
    )(flag, *flat, w0, w1)


def combine_y(kept, received, rows, width):
    a = ROWS_SUM

    def body(kept_ref, got, o1, o2, o3):
        k = pl.program_id(0)
        first = kept_ref[:a] + get(got, (0, slice(None)))
        for i, out in enumerate((o1, o2, o3)):

            @pl.when(k == i)
            def _(out=out):
                put(out, (slice(0, a),), first)
                put(out, (slice(a, rows),), kept_ref[a:])

    shape = (rows, width + LANES)
    return pl.pallas_call(
        body,
        grid=(3,),
        in_specs=[
            pl.BlockSpec((rows, width), lambda k: (k, 0)),
            pl.BlockSpec((1, a, width + LANES), lambda k: (k, 0, 0)),
        ],
        out_specs=[full(shape)] * 3,
        out_shape=[jax.ShapeDtypeStruct(shape, jnp.int16)] * 3,
        name="combine_y",
    )(kept, received)


def combine_x(kept, received, rows, width):
    a = ROWS_SUM

    def body(kept_ref, g1, g2, g3, out):
        last = kept_ref[a:] + get(g1, (slice(None),)) + get(g2, (slice(None),)) + get(g3, (slice(None),))
        put(out, (slice(0, a),), kept_ref[:a])
        put(out, (slice(a, rows),), last)

    shape = (rows, width + LANES)
    return pl.pallas_call(
        body,
        grid=(1,),
        in_specs=[pl.BlockSpec((rows, width), lambda k: (3, 0))]
        + [full(received[0].shape)] * 3,
        out_specs=full(shape),
        out_shape=jax.ShapeDtypeStruct(shape, jnp.int16),
        name="combine_x",
    )(kept, *received)


def finish(kept, received, labels, first_column, rows, width):
    def body(first_ref, kept_ref, g1, g2, g3, g4, label_ref, e_ref, stat_ref):
        logits = kept_ref[...]
        for g in (g1, g2, g3, g4):
            logits = logits + get(g, (slice(None),))
        columns = lax.broadcasted_iota(jnp.int32, (rows, width), 1) + first_ref[0]
        hit = columns == label_ref[:, :1]
        peak = jnp.max(logits, axis=1, keepdims=True)
        raised = jnp.exp(logits - peak)
        total = jnp.sum(raised, axis=1, keepdims=True)
        picked = jnp.sum(jnp.where(hit, logits, 0.0), axis=1, keepdims=True)
        e_ref[...] = raised.astype(BF16)
        lane = lax.broadcasted_iota(jnp.int32, (rows, LANES), 1)
        stat_ref[...] = jnp.where(lane == 0, peak, jnp.where(lane == 1, total, picked))

    return pl.pallas_call(
        body,
        grid=(1,),
        in_specs=[
            pl.BlockSpec(memory_space=pltpu.SMEM),
            pl.BlockSpec((rows, width), lambda k: (4, 0)),
        ]
        + [full(received[0].shape)] * 4
        + [full((rows, LANES))],
        out_specs=[full((rows, width)), full((rows, LANES))],
        out_shape=[
            jax.ShapeDtypeStruct((rows, width), BF16),
            jax.ShapeDtypeStruct((rows, LANES), F32),
        ],
        name="finish",
    )(first_column, kept, *received, labels)


def slopes(pieces, scale, label, first_column, width):
    sizes = [p.shape[0] for p in pieces]
    total = sum(sizes)

    def body(first_ref, *refs):
        ins, scale_ref, label_ref, out = refs[:-3], refs[-3], refs[-2], refs[-1]
        columns = lax.broadcasted_iota(jnp.int32, (sizes[0], width), 1) + first_ref[0]
        at = 0
        for ref, n in zip(ins, sizes):
            hit = columns[:n] == label_ref[at : at + n, :1]
            value = ref[...].astype(F32) * scale_ref[at : at + n, :1]
            out[at : at + n] = (value - jnp.where(hit, 1.0, 0.0)).astype(BF16)
            at += n

    return pl.pallas_call(
        body,
        grid=(1,),
        in_specs=[pl.BlockSpec(memory_space=pltpu.SMEM)]
        + [full(p.shape) for p in pieces]
        + [full((total, LANES))] * 2,
        out_specs=full((total, width)),
        out_shape=jax.ShapeDtypeStruct((total, width), BF16),
    )(first_column, *pieces, scale, label)


def pieces_of(hidden, starts, depth):
    count = len(starts) // 2
    rows = hidden.shape[0]

    def body(at_ref, source, *refs):
        outs, sems = refs[:count], refs[count]
        copies = []
        for k in range(2 * count):
            at = pl.multiple_of(at_ref[k] * depth, LANES)
            copies.append(
                pltpu.make_async_copy(
                    source.at[:, pl.ds(at, depth)],
                    outs[k // 2].at[:, pl.ds((k % 2) * depth, depth)],
                    sems.at[k],
                )
            )
        for copy in copies:
            copy.start()
        for copy in copies:
            copy.wait()

    return pl.pallas_call(
        body,
        in_specs=[pl.BlockSpec(memory_space=pltpu.SMEM), pl.BlockSpec(memory_space=pl.ANY)],
        out_specs=[pl.BlockSpec(memory_space=pl.ANY)] * count,
        out_shape=[jax.ShapeDtypeStruct((rows, 2 * depth), BF16)] * count,
        scratch_shapes=[pltpu.SemaphoreType.DMA((2 * count,))],
        name="pieces",
    )(jnp.stack(starts).astype(jnp.int32), hidden)


def gradient(turned, slope, other, before):
    depth, double = turned.shape
    n, width = slope.shape
    block = width // STEPS

    def body(turned_ref, s_ref, o_ref, *refs):
        value = jnp.dot(turned_ref[:, :n], s_ref[...], preferred_element_type=F32)
        value += jnp.dot(turned_ref[:, n:], o_ref[...], preferred_element_type=F32)
        refs[-1][...] = value + refs[0][...] if len(refs) == 2 else value

    col = lambda r: pl.BlockSpec((r, block), lambda j: (0, j))
    extra = () if before is None else (before,)
    return pl.pallas_call(
        body,
        grid=(STEPS,),
        in_specs=[full((depth, double)), col(n), col(n)] + [col(depth)] * len(extra),
        out_specs=col(depth),
        out_shape=jax.ShapeDtypeStruct((depth, width), F32),
    )(turned, slope, other, *extra)


def per_device(hidden, head_weight, targets):
    here = lax.axis_index("dp")
    block_index = lax.axis_index("vocab")
    c = here % C
    x = (here // C) % X
    y = here // (C * X)
    odd = block_index % 2
    rows = hidden.shape[0]
    depth, width = head_weight.shape

    partner_weight = from_core(head_weight)

    def columns_for(dy, dx):
        chip = ((y - dy) % Y) * X + (x ^ dx)
        return [chip * C + c, chip * C + 1 - c]

    wanted = [columns_for(1, odd), columns_for(3, 1 - odd), columns_for(2, odd)]
    wanted += [columns_for(0, 1), columns_for(0, 0)]
    p1, p3, p2, p0, own = pieces_of(hidden, [v for w in wanted for v in w], depth)

    def direct(piece, dy, outer):
        def source(y, x, c, h, z):
            s = side(dy, z)
            return (y + dy, x ^ s, c, h ^ (s if outer else 0), z)

        return fetch(piece, source)

    near = {1: direct(p1, 1, True), 3: direct(p3, 3, True)}
    near[2] = direct(p2, 2, False)
    across = from_x(p0)
    half = rows // 2
    far = {
        1: [from_z(near[1], -1)],
        3: [from_z(near[3], 1)],
        2: [from_z(near[2][:half], -1), from_z(near[2][half:], 1)],
    }
    flag = odd.reshape(1).astype(jnp.int32)
    weights = (head_weight, partner_weight)

    to_x, *to_y = products(flag, near, far, [], weights, True)
    got_x = from_x(to_x)
    got_y = [from_y(v, -dy) for v, dy in zip(to_y, (1, 2, 3))]
    kept, token = products(flag, near, far, [across, own], weights, False)
    send_y = combine_y(kept, got_x, rows, width)
    send_x = combine_x(kept, got_y, rows, width)
    received = [from_x(send_x)]
    received += [from_y(v, -dy) for v, dy in zip(send_y, (1, 2, 3))]

    token = token[0, 0]
    targets = targets + token
    later = odd + token
    first_column = (block_index * width).reshape(1).astype(jnp.int32)
    labels = lax.dynamic_slice_in_dim(targets, here * rows, rows, 0)
    spread = lambda v: jnp.broadcast_to(v[:, None], (v.shape[0], LANES))
    raised, stats = finish(kept, received, spread(labels), first_column, rows, width)

    g = ROWS_OUT
    side_x = from_x(raised)
    along = {dy: from_y(raised, dy) for dy in (2, 1, 3)}
    far_y = {dy: from_y(side_x[g:], dy) for dy in (2, 1, 3)}
    far_x = {dy: from_x(along[dy][:g]) for dy in (1, 3, 2)}

    stats = stats[:, :3].T
    every = lax.all_to_all(
        jnp.broadcast_to(stats[None], (16, *stats.shape)), "vocab", 0, 0, tiled=True
    )
    top = jnp.max(every[:, 0], axis=0)
    total = jnp.sum(every[:, 1] * jnp.exp(every[:, 0] - top[None]), axis=0)
    loss = top + jnp.log(total) - jnp.sum(every[:, 2], axis=0)
    factor = jnp.exp(stats[0] - top) / total
    factors = lax.all_to_all(
        jnp.broadcast_to(factor[None], (16, rows)), "dp", 0, 0, tiled=True
    )

    ids = targets.reshape(16, rows)

    def pick(table, dy, dx, a, b):
        owner = (((y + dy) % Y) * X + (x ^ dx)) * C + c
        return lax.dynamic_index_in_dim(table, owner, 0, keepdims=False)[a:b]

    def both(spans):
        return [
            spread(jnp.concatenate([pick(t, *s) for s in spans])) for t in (factors, ids)
        ]

    def states(dy, dx):
        if dy == 0:
            return across if dx else own
        whole = jnp.concatenate(far[dy], axis=0)
        return jnp.where((later if dy != 3 else 1 - later) == dx, near[dy], whole)

    def gathered(spans):
        whole = jnp.concatenate([states(dy, dx)[a:b] for dy, dx, a, b in spans], axis=0)
        whole = whole + token.astype(BF16)
        other = from_core(whole[:, depth:])
        return jnp.concatenate([whole[:, :depth], other], axis=0).T

    near_spans = [(dy, 0, 0, rows) for dy in range(Y)] + [(0, 1, 0, rows)]
    far_spans = [(dy, 1, 0, g) for dy in (1, 2, 3)] + [(dy, 1, g, rows) for dy in (1, 2, 3)]
    near_states = gathered(near_spans)
    far_states = gathered(far_spans)
    slope_near = slopes(
        [raised, along[1], along[2], along[3], side_x],
        *both(near_spans), first_column, width,
    )
    slope_far = slopes(
        [far_x[d] for d in (1, 2, 3)] + [far_y[d] for d in (1, 2, 3)],
        *both(far_spans), first_column, width,
    )
    near_other = from_core(slope_near)
    far_other = from_core(slope_far)
    grad = gradient(near_states, slope_near, near_other, None)
    grad = gradient(far_states, slope_far, far_other, grad)
    return (loss, grad)


def solution(mesh):
    in_specs = (P("dp", None), P("dp", "vocab"), P())
    out_specs = (P("dp"), P("dp", "vocab"))

    return jax.shard_map(
        per_device, mesh=mesh, in_specs=in_specs, out_specs=out_specs, check_vma=False
    )
```

```python
import jax
import jax.numpy as jnp
from jax import lax
from jax.experimental import pallas as pl
from jax.experimental.pallas import tpu as pltpu
from jax.sharding import PartitionSpec as P


AXES = ("dp", "vocab")
Y, X, C, H, Z = 4, 2, 2, 2, 8
LANES = 128
ROWS_SUM = 48
ROWS_OUT = 80
F32, BF16 = jnp.float32, jnp.bfloat16


def device(y, x, c, h, z):
    return ((((y % Y) * X + x) * C + c) * H + h) * Z + z % Z


def fetch(value, source):
    pairs = [
        (device(*source(y, x, c, h, z)), device(y, x, c, h, z))
        for y in range(Y)
        for x in range(X)
        for c in range(C)
        for h in range(H)
        for z in range(Z)
    ]
    return lax.ppermute(value, AXES, pairs)


def from_y(value, dy):
    return fetch(value, lambda y, x, c, h, z: (y + dy, x, c, h, z))


def from_x(value):
    return fetch(value, lambda y, x, c, h, z: (y, x ^ 1, c, h, z))


def from_z(value, dz):
    return fetch(value, lambda y, x, c, h, z: (y, x, c, h, z + dz))


def from_core(value):
    return fetch(value, lambda y, x, c, h, z: (y, x, c ^ 1, h, z))


def encode(values):
    peak = jnp.max(jnp.abs(values), axis=-1, keepdims=True)
    power = jnp.ceil(jnp.log2(jnp.maximum(peak, 1e-30) * (1.0 / 32000.0)))
    codes = jnp.round(values * jnp.exp2(-power)).astype(jnp.int32).astype(jnp.int16)
    tail = jnp.broadcast_to(power, (values.shape[0], LANES)).astype(jnp.int32)
    return codes, tail.astype(jnp.int16)


def put(ref, index, values):
    width = values.shape[-1]
    codes, tail = encode(values)
    ref[(*index, slice(0, width))] = codes
    ref[(*index, slice(width, width + LANES))] = tail


def get(ref, index):
    width = ref.shape[-1] - LANES
    power = ref[(*index, slice(width, width + LANES))].astype(jnp.int32).astype(F32)
    codes = ref[(*index, slice(0, width))].astype(jnp.int32).astype(F32)
    return codes * jnp.exp2(power[:, :1])


def rows_of(pieces, flag, dy, dx):
    if dy != 2:
        return pieces[dy, dx][...]
    far = jnp.concatenate([f[...] for f in pieces["far"]], axis=0)
    return jnp.where(flag == dx, pieces["near"][...], far)


def full(shape):
    return pl.BlockSpec(shape, lambda j: (0,) * len(shape))


STEPS = 4
NEAR = ((0, 0), (1, 0), (2, 0), (3, 0), (0, 1))
FAR = ((1, 1), (2, 1), (3, 1))


def partial_call(flag, pieces, keys, weights, out_shape, out_specs, finish_step):
    w0, w1 = weights
    depth, width = w0.shape
    block = width // STEPS
    names = [k for k in pieces if k in keys or (k in ("near", "far") and any(q[0] == 2 for q in keys))]
    flat = []
    for k in names:
        flat += pieces[k] if k == "far" else [pieces[k]]
    rows = pieces[1, 1].shape[0]
    total = len(keys) * rows

    def body(flag_ref, *refs):
        refs = list(refs)
        by = {}
        for k in names:
            by[k] = [refs.pop(0), refs.pop(0)] if k == "far" else refs.pop(0)
        w0_ref, w1_ref = refs[:2]
        outs, left, acc = refs[2:-2], refs[-2], refs[-1]
        j = pl.program_id(0)

        @pl.when(j == 0)
        def _():
            for n, (dy, dx) in enumerate(keys):
                left[n * rows : (n + 1) * rows] = rows_of(by, flag_ref[0], dy, dx)

        value = jnp.dot(left[:, :depth], w0_ref[...], preferred_element_type=F32)
        value += jnp.dot(left[:, depth:], w1_ref[...], preferred_element_type=F32)
        finish_step(j, value, outs, acc)

    return pl.pallas_call(
        body,
        grid=(STEPS,),
        in_specs=[pl.BlockSpec(memory_space=pltpu.SMEM)]
        + [full(v.shape) for v in flat]
        + [pl.BlockSpec((depth, block), lambda j: (0, j))] * 2,
        out_specs=out_specs,
        out_shape=out_shape,
        scratch_shapes=[
            pltpu.VMEM((total, 2 * depth), BF16),
            pltpu.VMEM((STEPS, total, block), F32),
        ],
    )(flag, *flat, w0, w1)


def sends(flag, pieces, weights, rows, width):
    a = ROWS_SUM
    shapes = [(3, a, width + LANES)] + [(rows - a, width + LANES)] * 3

    def step(j, value, outs, acc):
        acc[j] = value

        @pl.when(j == STEPS - 1)
        def _():
            for k in range(3):
                whole = jnp.concatenate(
                    [acc[s, k * rows : (k + 1) * rows] for s in range(STEPS)], axis=1
                )
                put(outs[0], (k, slice(None)), whole[:a])
                put(outs[1 + k], (slice(None),), whole[a:])

    return partial_call(
        flag, pieces, FAR, weights,
        [jax.ShapeDtypeStruct(s, jnp.int16) for s in shapes],
        [full(s) for s in shapes], step,
    )


KEPT = ((1, 0), (2, 0), (3, 0), (0, 1), (0, 0))


def keeps(flag, pieces, weights, rows, width):
    total = len(KEPT) * rows

    def step(j, value, outs, acc):
        outs[0][...] = value

    return partial_call(
        flag, pieces, KEPT, weights,
        jax.ShapeDtypeStruct((total, width), F32),
        pl.BlockSpec((total, width // STEPS), lambda j: (0, j)), step,
    )


def combine_y(kept, received, rows, width):
    a = ROWS_SUM

    def body(kept_ref, got, o1, o2, o3):
        k = pl.program_id(0)
        first = kept_ref[:a] + get(got, (0, slice(None)))
        for i, out in enumerate((o1, o2, o3)):

            @pl.when(k == i)
            def _(out=out):
                put(out, (slice(0, a),), first)
                put(out, (slice(a, rows),), kept_ref[a:])

    shape = (rows, width + LANES)
    return pl.pallas_call(
        body,
        grid=(3,),
        in_specs=[
            pl.BlockSpec((rows, width), lambda k: (k, 0)),
            pl.BlockSpec((1, a, width + LANES), lambda k: (k, 0, 0)),
        ],
        out_specs=[full(shape)] * 3,
        out_shape=[jax.ShapeDtypeStruct(shape, jnp.int16)] * 3,
        name="combine_y",
    )(kept, received)


def combine_x(kept, received, rows, width):
    a = ROWS_SUM

    def body(kept_ref, g1, g2, g3, out, token):
        last = kept_ref[a:] + get(g1, (slice(None),)) + get(g2, (slice(None),)) + get(g3, (slice(None),))
        put(out, (slice(0, a),), kept_ref[:a])
        put(out, (slice(a, rows),), last)
        token[...] = jnp.zeros((8, LANES), jnp.int32)

    shape = (rows, width + LANES)
    return pl.pallas_call(
        body,
        grid=(1,),
        in_specs=[pl.BlockSpec((rows, width), lambda k: (3, 0))]
        + [full(received[0].shape)] * 3,
        out_specs=[full(shape), full((8, LANES))],
        out_shape=[
            jax.ShapeDtypeStruct(shape, jnp.int16),
            jax.ShapeDtypeStruct((8, LANES), jnp.int32),
        ],
        name="combine_x",
    )(kept, *received)


def upright(line):
    return jnp.transpose(jnp.broadcast_to(line, (LANES, LANES)))


def finish(kept, received, ids, place, rows, width):
    def body(place_ref, kept_ref, g1, g2, g3, g4, ids_ref, e_ref, stat_ref):
        logits = kept_ref[...]
        for g in (g1, g2, g3, g4):
            logits = logits + get(g, (slice(None),))
        columns = lax.broadcasted_iota(jnp.int32, (rows, width), 1) + place_ref[1]
        label = upright(ids_ref[pl.ds(place_ref[0], 1), :])
        hit = columns.astype(F32) == label[:, :1]
        peak = jnp.max(logits, axis=1, keepdims=True)
        raised = jnp.exp(logits - peak)
        total = jnp.sum(raised, axis=1, keepdims=True)
        picked = jnp.sum(jnp.where(hit, logits, 0.0), axis=1, keepdims=True)
        e_ref[...] = raised.astype(BF16)
        lines = [jnp.transpose(jnp.broadcast_to(v, (rows, LANES)))[:1] for v in (peak, total, picked)]
        lines = jnp.concatenate(lines + [jnp.zeros((5, rows), F32)], axis=0)
        for k in range(16):
            stat_ref[k] = lines

    return pl.pallas_call(
        body,
        grid=(1,),
        in_specs=[
            pl.BlockSpec(memory_space=pltpu.SMEM),
            pl.BlockSpec((rows, width), lambda k: (4, 0)),
        ]
        + [full(received[0].shape)] * 4
        + [full(ids.shape)],
        out_specs=[full((rows, width)), full((16, 8, rows))],
        out_shape=[
            jax.ShapeDtypeStruct((rows, width), BF16),
            jax.ShapeDtypeStruct((16, 8, rows), F32),
        ],
        name="finish",
    )(place, kept, *received, ids)


def settle(every, stats):
    def body(every_ref, own_ref, loss_ref, factor_ref):
        peaks, totals, picks = (every_ref[:, k] for k in range(3))
        top = jnp.max(peaks, axis=0, keepdims=True)
        total = jnp.sum(totals * jnp.exp(peaks - top), axis=0, keepdims=True)
        picked = jnp.sum(picks, axis=0, keepdims=True)
        loss_ref[...] = top + jnp.log(total) - picked
        factor = jnp.exp(own_ref[0, :1] - top) / total
        factor_ref[...] = jnp.broadcast_to(factor[None], factor_ref.shape)

    rows = every.shape[-1]
    return pl.pallas_call(
        body,
        out_shape=[
            jax.ShapeDtypeStruct((1, rows), F32),
            jax.ShapeDtypeStruct(every.shape, F32),
        ],
        name="settle",
    )(every, stats)


def slopes(pieces, spans, factors, ids, place, width):
    sizes = [p.shape[0] for p in pieces]
    total = sum(sizes)

    def body(place_ref, *refs):
        ins, factor_ref, ids_ref, out = refs[:-3], refs[-3], refs[-2], refs[-1]
        columns = lax.broadcasted_iota(jnp.int32, (max(sizes), width), 1) + place_ref[1]
        columns = columns.astype(F32)
        at = 0
        for ref, n, (k, a, b) in zip(ins, sizes, spans):
            owner = place_ref[2 + k]
            scale = upright(factor_ref[owner, :1])[a:b, :1]
            label = upright(ids_ref[pl.ds(owner, 1), :])[a:b, :1]
            value = ref[...].astype(F32) * scale
            value = value - jnp.where(columns[:n] == label, 1.0, 0.0)
            out[at : at + n] = value.astype(BF16)
            at += n

    return pl.pallas_call(
        body,
        grid=(1,),
        in_specs=[pl.BlockSpec(memory_space=pltpu.SMEM)]
        + [full(p.shape) for p in pieces]
        + [full(factors.shape), full(ids.shape)],
        out_specs=full((total, width)),
        out_shape=jax.ShapeDtypeStruct((total, width), BF16),
    )(place, *pieces, factors, ids)


def turned(flag, pieces, rows, depth):
    g = ROWS_OUT
    names = list(pieces)
    flat = []
    for k in names:
        flat += pieces[k] if k == "far" else [pieces[k]]

    def body(flag_ref, *refs):
        refs = list(refs)
        by = {}
        for k in names:
            by[k] = [refs.pop(0), refs.pop(0)] if k == "far" else refs.pop(0)
        mine, theirs = refs
        near = [rows_of(by, flag_ref[0], dy, dx) for dy, dx in NEAR]
        far = [rows_of(by, flag_ref[0], dy, dx) for dy, dx in FAR]
        far = jnp.concatenate([f[:g] for f in far] + [f[g:] for f in far], axis=0)
        parts = near + [far[k * rows : (k + 1) * rows] for k in range(3)]
        for k, part in enumerate(parts):
            flipped = jnp.transpose(part)
            mine[:, k * rows : (k + 1) * rows] = flipped[:depth]
            theirs[:, k * rows : (k + 1) * rows] = flipped[depth:]

    shape = (depth, 8 * rows)
    return pl.pallas_call(
        body,
        grid=(1,),
        in_specs=[pl.BlockSpec(memory_space=pltpu.SMEM)] + [full(v.shape) for v in flat],
        out_specs=[full(shape)] * 2,
        out_shape=[jax.ShapeDtypeStruct(shape, BF16)] * 2,
        name="turned",
    )(flag, *flat)


def gradient(mine, theirs, near, near_other, far, far_other):
    depth = mine.shape[0]
    n, width = near.shape
    block = width // STEPS

    def body(m_ref, t_ref, a_ref, b_ref, c_ref, d_ref, out):
        value = jnp.dot(m_ref[:, :n], a_ref[...], preferred_element_type=F32)
        value += jnp.dot(t_ref[:, :n], b_ref[...], preferred_element_type=F32)
        value += jnp.dot(m_ref[:, n:], c_ref[...], preferred_element_type=F32)
        value += jnp.dot(t_ref[:, n:], d_ref[...], preferred_element_type=F32)
        out[...] = value

    col = lambda r: pl.BlockSpec((r, block), lambda j: (0, j))
    m = far.shape[0]
    return pl.pallas_call(
        body,
        grid=(STEPS,),
        in_specs=[full(mine.shape)] * 2 + [col(n)] * 2 + [col(m)] * 2,
        out_specs=col(depth),
        out_shape=jax.ShapeDtypeStruct((depth, width), F32),
        name="gradient",
    )(mine, theirs, near, near_other, far, far_other)


def per_device(hidden, head_weight, targets):
    here = lax.axis_index("dp")
    block_index = lax.axis_index("vocab")
    c = here % C
    x = (here // C) % X
    y = here // (C * X)
    odd = block_index % 2
    rows = hidden.shape[0]
    depth, width = head_weight.shape

    def columns_for(dy, dx):
        chip = ((y - dy) % Y) * X + (x ^ dx)
        own = lax.dynamic_slice_in_dim(hidden, (chip * C + c) * depth, depth, 1)
        other = lax.dynamic_slice_in_dim(hidden, (chip * C + 1 - c) * depth, depth, 1)
        return jnp.concatenate([own, other], axis=1)

    def two_hop(y, x, c, h, z):
        return (y + 2, x ^ (z % 2), c, h, z)

    def outside(dy):
        return lambda y, x, c, h, z: (y + dy, x ^ 1, c, h ^ 1, z)

    half = rows // 2
    near2 = fetch(columns_for(2, odd), two_hop)
    pieces = {
        "near": near2,
        "far": [from_z(near2[:half], -1), from_z(near2[half:], 1)],
        (1, 1): fetch(columns_for(1, 1), outside(1)),
        (3, 1): fetch(columns_for(3, 1), outside(3)),
        (1, 0): from_y(columns_for(1, 0), 1),
        (3, 0): from_y(columns_for(3, 0), 3),
        (0, 1): from_x(columns_for(0, 1)),
        (0, 0): columns_for(0, 0),
    }
    flag = odd.reshape(1).astype(jnp.int32)
    weights = (head_weight, from_core(head_weight))

    to_x, *to_y = sends(flag, pieces, weights, rows, width)
    got_x = from_x(to_x)
    got_y = [from_y(v, -dy) for v, dy in zip(to_y, (1, 2, 3))]
    kept = keeps(flag, pieces, weights, rows, width)
    send_y = combine_y(kept, got_x, rows, width)
    send_x, token = combine_x(kept, got_y, rows, width)
    received = [from_x(send_x)]
    received += [from_y(v, -dy) for v, dy in zip(send_y, (1, 2, 3))]

    token = token[0, 0]
    mine, sent = turned(flag + token, pieces, rows, depth)
    theirs = from_core(sent)
    ids = (targets + token).astype(F32).reshape(16, rows)
    owners = [(((y + dy) % Y) * X + (x ^ dx)) * C + c for dy, dx in NEAR + FAR]
    place = jnp.stack([here, block_index * width, *owners]).astype(jnp.int32)
    raised, stats = finish(kept, received, ids, place, rows, width)

    g = ROWS_OUT
    side_x = from_x(raised)
    along = {dy: from_y(raised, dy) for dy in (2, 1, 3)}
    far_y = {dy: from_y(side_x[g:], dy) for dy in (2, 1, 3)}
    far_x = {dy: from_x(along[dy][:g]) for dy in (1, 3, 2)}

    every = lax.all_to_all(stats, "vocab", 0, 0, tiled=True)
    loss, factor = settle(every, stats)
    factors = lax.all_to_all(factor, "dp", 0, 0, tiled=True)

    near_spans = [(k, 0, rows) for k in range(5)]
    far_spans = [(5 + k, 0, g) for k in range(3)] + [(5 + k, g, rows) for k in range(3)]
    slope_near = slopes(
        [raised, along[1], along[2], along[3], side_x],
        near_spans, factors, ids, place, width,
    )
    slope_far = slopes(
        [far_x[d] for d in (1, 2, 3)] + [far_y[d] for d in (1, 2, 3)],
        far_spans, factors, ids, place, width,
    )
    near_other = from_core(slope_near)
    far_other = from_core(slope_far)
    grad = gradient(mine, theirs, slope_near, near_other, slope_far, far_other)
    return (loss.reshape(rows), grad)


def solution(mesh):
    in_specs = (P("dp", None), P("dp", "vocab"), P())
    out_specs = (P("dp"), P("dp", "vocab"))

    return jax.shard_map(
        per_device, mesh=mesh, in_specs=in_specs, out_specs=out_specs, check_vma=False
    )
```

```python
import jax
import jax.numpy as jnp
from jax import lax
from jax.experimental import pallas as pl
from jax.experimental.pallas import tpu as pltpu
from jax.sharding import PartitionSpec as P


AXES = ("dp", "vocab")
Y, X, C, H, Z = 4, 2, 2, 2, 8
LANES = 128
ROWS_SUM = 48
ROWS_OUT = 80
F32, BF16 = jnp.float32, jnp.bfloat16


def device(y, x, c, h, z):
    return ((((y % Y) * X + x) * C + c) * H + h) * Z + z % Z


def fetch(value, source):
    pairs = [
        (device(*source(y, x, c, h, z)), device(y, x, c, h, z))
        for y in range(Y)
        for x in range(X)
        for c in range(C)
        for h in range(H)
        for z in range(Z)
    ]
    return lax.ppermute(value, AXES, pairs)


def from_y(value, dy):
    return fetch(value, lambda y, x, c, h, z: (y + dy, x, c, h, z))


def from_x(value):
    return fetch(value, lambda y, x, c, h, z: (y, x ^ 1, c, h, z))


def from_core(value):
    return fetch(value, lambda y, x, c, h, z: (y, x, c ^ 1, h, z))


def encode(values):
    peak = jnp.max(jnp.abs(values), axis=-1, keepdims=True)
    power = jnp.ceil(jnp.log2(jnp.maximum(peak, 1e-30) * (1.0 / 32000.0)))
    codes = jnp.round(values * jnp.exp2(-power)).astype(jnp.int32).astype(jnp.int16)
    tail = jnp.broadcast_to(power, (values.shape[0], LANES)).astype(jnp.int32)
    return codes, tail.astype(jnp.int16)


def put(ref, index, values):
    width = values.shape[-1]
    codes, tail = encode(values)
    ref[(*index, slice(0, width))] = codes
    ref[(*index, slice(width, width + LANES))] = tail


def get(ref, index):
    width = ref.shape[-1] - LANES
    power = ref[(*index, slice(width, width + LANES))].astype(jnp.int32).astype(F32)
    codes = ref[(*index, slice(0, width))].astype(jnp.int32).astype(F32)
    return codes * jnp.exp2(power[:, :1])


def full(shape):
    return pl.BlockSpec(shape, lambda j: (0,) * len(shape))


STEPS = 4
NEAR = ((0, 0), (1, 0), (2, 0), (3, 0), (0, 1))
FAR = ((1, 1), (2, 1), (3, 1))


def partial_call(pieces, keys, weights, out_shape, out_specs, finish_step):
    w0, w1 = weights
    depth, width = w0.shape
    block = width // STEPS
    flat = [pieces[k] for k in keys]
    count = len(flat)
    rows = flat[0].shape[0]
    total = count * rows

    def body(*refs):
        w0_ref, w1_ref = refs[count : count + 2]
        outs, left, acc = refs[count + 2 : -2], refs[-2], refs[-1]
        j = pl.program_id(0)

        @pl.when(j == 0)
        def _():
            for n in range(count):
                left[n * rows : (n + 1) * rows] = refs[n][...]

        value = jnp.dot(left[:, :depth], w0_ref[...], preferred_element_type=F32)
        value += jnp.dot(left[:, depth:], w1_ref[...], preferred_element_type=F32)
        finish_step(j, value, outs, acc)

    return pl.pallas_call(
        body,
        grid=(STEPS,),
        in_specs=[full(v.shape) for v in flat]
        + [pl.BlockSpec((depth, block), lambda j: (0, j))] * 2,
        out_specs=out_specs,
        out_shape=out_shape,
        scratch_shapes=[
            pltpu.VMEM((total, 2 * depth), BF16),
            pltpu.VMEM((STEPS, total, block), F32),
        ],
    )(*flat, w0, w1)


def sends(pieces, weights, rows, width):
    a = ROWS_SUM
    shapes = [(3, a, width + LANES)] + [(rows - a, width + LANES)] * 3

    def step(j, value, outs, acc):
        acc[j] = value

        @pl.when(j == STEPS - 1)
        def _():
            for k in range(3):
                whole = jnp.concatenate(
                    [acc[s, k * rows : (k + 1) * rows] for s in range(STEPS)], axis=1
                )
                put(outs[0], (k, slice(None)), whole[:a])
                put(outs[1 + k], (slice(None),), whole[a:])

    return partial_call(
        pieces, FAR, weights,
        [jax.ShapeDtypeStruct(s, jnp.int16) for s in shapes],
        [full(s) for s in shapes], step,
    )


def keeps(pieces, keys, weights, width):
    total = len(keys) * pieces[keys[0]].shape[0]

    def step(j, value, outs, acc):
        outs[0][...] = value

    return partial_call(
        pieces, keys, weights,
        jax.ShapeDtypeStruct((total, width), F32),
        pl.BlockSpec((total, width // STEPS), lambda j: (0, j)), step,
    )


def combine_y(kept, received, rows, width):
    a = ROWS_SUM

    def body(kept_ref, got, o1, o2, o3):
        k = pl.program_id(0)
        first = kept_ref[:a] + get(got, (0, slice(None)))
        for i, out in enumerate((o1, o2, o3)):

            @pl.when(k == i)
            def _(out=out):
                put(out, (slice(0, a),), first)
                put(out, (slice(a, rows),), kept_ref[a:])

    shape = (rows, width + LANES)
    return pl.pallas_call(
        body,
        grid=(3,),
        in_specs=[
            pl.BlockSpec((rows, width), lambda k: (k, 0)),
            pl.BlockSpec((1, a, width + LANES), lambda k: (k, 0, 0)),
        ],
        out_specs=[full(shape)] * 3,
        out_shape=[jax.ShapeDtypeStruct(shape, jnp.int16)] * 3,
        name="combine_y",
    )(kept, received)


def combine_x(kept, received, rows, width):
    a = ROWS_SUM

    def body(kept_ref, g1, g2, g3, out, token):
        last = kept_ref[a:] + get(g1, (slice(None),)) + get(g2, (slice(None),)) + get(g3, (slice(None),))
        put(out, (slice(0, a),), kept_ref[:a])
        put(out, (slice(a, rows),), last)
        token[...] = jnp.zeros((8, LANES), jnp.int32)

    shape = (rows, width + LANES)
    return pl.pallas_call(
        body,
        grid=(1,),
        in_specs=[pl.BlockSpec((rows, width), lambda k: (0, 0))]
        + [full(received[0].shape)] * 3,
        out_specs=[full(shape), full((8, LANES))],
        out_shape=[
            jax.ShapeDtypeStruct(shape, jnp.int16),
            jax.ShapeDtypeStruct((8, LANES), jnp.int32),
        ],
        name="combine_x",
    )(kept, *received)


def upright(line):
    return jnp.transpose(jnp.broadcast_to(line, (LANES, LANES)))


def finish(kept, received, ids, place, rows, width):
    def body(place_ref, kept_ref, g1, g2, g3, g4, ids_ref, e_ref, stat_ref):
        logits = kept_ref[...]
        for g in (g1, g2, g3, g4):
            logits = logits + get(g, (slice(None),))
        columns = lax.broadcasted_iota(jnp.int32, (rows, width), 1) + place_ref[1]
        label = upright(ids_ref[pl.ds(place_ref[0], 1), :])
        hit = columns.astype(F32) == label[:, :1]
        peak = jnp.max(logits, axis=1, keepdims=True)
        raised = jnp.exp(logits - peak)
        total = jnp.sum(raised, axis=1, keepdims=True)
        picked = jnp.sum(jnp.where(hit, logits, 0.0), axis=1, keepdims=True)
        e_ref[...] = raised.astype(BF16)
        lines = [jnp.transpose(jnp.broadcast_to(v, (rows, LANES)))[:1] for v in (peak, total, picked)]
        lines = jnp.concatenate(lines + [jnp.zeros((5, rows), F32)], axis=0)
        for k in range(16):
            stat_ref[k] = lines

    return pl.pallas_call(
        body,
        grid=(1,),
        in_specs=[
            pl.BlockSpec(memory_space=pltpu.SMEM),
            pl.BlockSpec((rows, width), lambda k: (1, 0)),
        ]
        + [full(received[0].shape)] * 4
        + [full(ids.shape)],
        out_specs=[full((rows, width)), full((16, 8, rows))],
        out_shape=[
            jax.ShapeDtypeStruct((rows, width), BF16),
            jax.ShapeDtypeStruct((16, 8, rows), F32),
        ],
        name="finish",
    )(place, kept, *received, ids)


def settle(every, stats):
    def body(every_ref, own_ref, loss_ref, factor_ref):
        peaks, totals, picks = (every_ref[:, k] for k in range(3))
        top = jnp.max(peaks, axis=0, keepdims=True)
        total = jnp.sum(totals * jnp.exp(peaks - top), axis=0, keepdims=True)
        picked = jnp.sum(picks, axis=0, keepdims=True)
        loss_ref[...] = top + jnp.log(total) - picked
        factor = jnp.exp(own_ref[0, :1] - top) / total
        factor_ref[...] = jnp.broadcast_to(factor[None], factor_ref.shape)

    rows = every.shape[-1]
    return pl.pallas_call(
        body,
        out_shape=[
            jax.ShapeDtypeStruct((1, rows), F32),
            jax.ShapeDtypeStruct(every.shape, F32),
        ],
        name="settle",
    )(every, stats)


def slopes(pieces, spans, factors, ids, place, width):
    sizes = [p.shape[0] for p in pieces]
    total = sum(sizes)

    def body(place_ref, *refs):
        ins, factor_ref, ids_ref, out = refs[:-3], refs[-3], refs[-2], refs[-1]
        columns = lax.broadcasted_iota(jnp.int32, (max(sizes), width), 1) + place_ref[1]
        columns = columns.astype(F32)
        at = 0
        for ref, n, (k, a, b) in zip(ins, sizes, spans):
            owner = place_ref[2 + k]
            scale = upright(factor_ref[owner, :1])[a:b, :1]
            label = upright(ids_ref[pl.ds(owner, 1), :])[a:b, :1]
            value = ref[...].astype(F32) * scale
            value = value - jnp.where(columns[:n] == label, 1.0, 0.0)
            out[at : at + n] = value.astype(BF16)
            at += n

    return pl.pallas_call(
        body,
        grid=(1,),
        in_specs=[pl.BlockSpec(memory_space=pltpu.SMEM)]
        + [full(p.shape) for p in pieces]
        + [full(factors.shape), full(ids.shape)],
        out_specs=full((total, width)),
        out_shape=jax.ShapeDtypeStruct((total, width), BF16),
    )(place, *pieces, factors, ids)


def turned(token, pieces, rows, depth):
    g = ROWS_OUT
    flat = [pieces[k] for k in NEAR + FAR]

    def body(token_ref, *refs):
        ins, (mine, theirs) = refs[:8], refs[8:]
        far = [r[...] for r in ins[5:]]
        far = jnp.concatenate([f[:g] for f in far] + [f[g:] for f in far], axis=0)
        parts = [r[...] for r in ins[:5]] + [far[k * rows : (k + 1) * rows] for k in range(3)]
        for k, part in enumerate(parts):
            flipped = jnp.transpose(part)
            mine[:, k * rows : (k + 1) * rows] = flipped[:depth]
            theirs[:, k * rows : (k + 1) * rows] = flipped[depth:]

    shape = (depth, 8 * rows)
    return pl.pallas_call(
        body,
        grid=(1,),
        in_specs=[full(token.shape)] + [full(v.shape) for v in flat],
        out_specs=[full(shape)] * 2,
        out_shape=[jax.ShapeDtypeStruct(shape, BF16)] * 2,
        name="turned",
    )(token, *flat)


def gradient(mine, theirs, near, near_other, far, far_other):
    depth = mine.shape[0]
    n, width = near.shape
    m = far.shape[0]
    block = width // (2 * STEPS)

    def body(m_ref, t_ref, a_ref, b_ref, c_ref, d_ref, out):
        own = jnp.concatenate([a_ref[...], c_ref[...]], axis=0)
        other = jnp.concatenate([b_ref[...], d_ref[...]], axis=0)
        value = jnp.dot(m_ref[...], own, preferred_element_type=F32)
        out[...] = value + jnp.dot(t_ref[...], other, preferred_element_type=F32)

    col = lambda r: pl.BlockSpec((r, block), lambda j: (0, j))
    return pl.pallas_call(
        body,
        grid=(2 * STEPS,),
        in_specs=[full(mine.shape)] * 2 + [col(n)] * 2 + [col(m)] * 2,
        out_specs=col(depth),
        out_shape=jax.ShapeDtypeStruct((depth, width), F32),
        name="gradient",
    )(mine, theirs, near, near_other, far, far_other)


def per_device(hidden, head_weight, targets):
    here = lax.axis_index("dp")
    block_index = lax.axis_index("vocab")
    c = here % C
    x = (here // C) % X
    y = here // (C * X)
    rows = hidden.shape[0]
    depth, width = head_weight.shape

    def columns_for(dy, dx):
        chip = ((y - dy) % Y) * X + (x ^ dx)
        own = lax.dynamic_slice_in_dim(hidden, (chip * C + c) * depth, depth, 1)
        other = lax.dynamic_slice_in_dim(hidden, (chip * C + 1 - c) * depth, depth, 1)
        return jnp.concatenate([own, other], axis=1)

    def outside(dy):
        return lambda y, x, c, h, z: (y + dy, x ^ 1, c, h ^ 1, z)

    weights = (head_weight, from_core(head_weight))
    pieces = {
        (2, 1): fetch(columns_for(2, 1), lambda y, x, c, h, z: (y + 2, x ^ 1, c, h, z)),
        (1, 1): fetch(columns_for(1, 1), outside(1)),
        (3, 1): fetch(columns_for(3, 1), outside(3)),
        (2, 0): from_y(columns_for(2, 0), 2),
        (1, 0): from_y(columns_for(1, 0), 1),
        (3, 0): from_y(columns_for(3, 0), 3),
        (0, 1): from_x(columns_for(0, 1)),
        (0, 0): columns_for(0, 0),
    }

    to_x, *to_y = sends(pieces, weights, rows, width)
    got_x = from_x(to_x)
    got_y = [from_y(v, -dy) for v, dy in zip(to_y, (1, 2, 3))]
    kept_y = keeps(pieces, NEAR[1:4], weights, width)
    kept_x = keeps(pieces, (NEAR[4], NEAR[0]), weights, width)
    send_y = combine_y(kept_y, got_x, rows, width)
    send_x, token = combine_x(kept_x, got_y, rows, width)
    received = [from_x(send_x)]
    received += [from_y(v, -dy) for v, dy in zip(send_y, (1, 2, 3))]

    mine, sent = turned(token, pieces, rows, depth)
    token = token[0, 0]
    theirs = from_core(sent)
    ids = (targets + token).astype(F32).reshape(16, rows)
    owners = [(((y + dy) % Y) * X + (x ^ dx)) * C + c for dy, dx in NEAR + FAR]
    place = jnp.stack([here, block_index * width, *owners]).astype(jnp.int32)
    raised, stats = finish(kept_x, received, ids, place, rows, width)

    g = ROWS_OUT
    side_x = from_x(raised)
    along = {dy: from_y(raised, dy) for dy in (2, 1, 3)}
    far_y = {dy: from_y(side_x[g:], dy) for dy in (2, 1, 3)}
    far_x = {dy: from_x(along[dy][:g]) for dy in (1, 3, 2)}

    every = lax.all_to_all(stats, "vocab", 0, 0, tiled=True)
    loss, factor = settle(every, stats)
    factors = lax.all_to_all(factor, "dp", 0, 0, tiled=True)

    near_spans = [(k, 0, rows) for k in range(5)]
    far_spans = [(5 + k, 0, g) for k in range(3)] + [(5 + k, g, rows) for k in range(3)]
    slope_near = slopes(
        [raised, along[1], along[2], along[3], side_x],
        near_spans, factors, ids, place, width,
    )
    slope_far = slopes(
        [far_x[d] for d in (1, 2, 3)] + [far_y[d] for d in (1, 2, 3)],
        far_spans, factors, ids, place, width,
    )
    near_other = from_core(slope_near)
    far_other = from_core(slope_far)
    grad = gradient(mine, theirs, slope_near, near_other, slope_far, far_other)
    return (loss.reshape(rows), grad)


def solution(mesh):
    in_specs = (P("dp", None), P("dp", "vocab"), P())
    out_specs = (P("dp"), P("dp", "vocab"))

    return jax.shard_map(
        per_device, mesh=mesh, in_specs=in_specs, out_specs=out_specs, check_vma=False
    )
```

```python
import jax
import jax.numpy as jnp
from jax import lax
from jax.experimental import pallas as pl
from jax.experimental.pallas import tpu as pltpu
from jax.sharding import PartitionSpec as P


AXES = ("dp", "vocab")
Y, X, C, H, Z = 4, 2, 2, 2, 8
LANES = 128
ROWS_SUM = 48
ROWS_OUT = 80
F32, BF16 = jnp.float32, jnp.bfloat16


def device(y, x, c, h, z):
    return ((((y % Y) * X + x) * C + c) * H + h) * Z + z % Z


def fetch(value, source):
    pairs = [
        (device(*source(y, x, c, h, z)), device(y, x, c, h, z))
        for y in range(Y)
        for x in range(X)
        for c in range(C)
        for h in range(H)
        for z in range(Z)
    ]
    return lax.ppermute(value, AXES, pairs)


def from_y(value, dy):
    return fetch(value, lambda y, x, c, h, z: (y + dy, x, c, h, z))


def from_x(value):
    return fetch(value, lambda y, x, c, h, z: (y, x ^ 1, c, h, z))


def from_core(value):
    return fetch(value, lambda y, x, c, h, z: (y, x, c ^ 1, h, z))


def encode(values):
    peak = jnp.max(jnp.abs(values), axis=-1, keepdims=True)
    power = jnp.ceil(jnp.log2(jnp.maximum(peak, 1e-30) * (1.0 / 32000.0)))
    codes = jnp.round(values * jnp.exp2(-power)).astype(jnp.int32).astype(jnp.int16)
    tail = jnp.broadcast_to(power, (values.shape[0], LANES)).astype(jnp.int32)
    return codes, tail.astype(jnp.int16)


def put(ref, index, values):
    width = values.shape[-1]
    codes, tail = encode(values)
    ref[(*index, slice(0, width))] = codes
    ref[(*index, slice(width, width + LANES))] = tail


def get(ref, index):
    width = ref.shape[-1] - LANES
    power = ref[(*index, slice(width, width + LANES))].astype(jnp.int32).astype(F32)
    codes = ref[(*index, slice(0, width))].astype(jnp.int32).astype(F32)
    return codes * jnp.exp2(power[:, :1])


def full(shape):
    return pl.BlockSpec(shape, lambda j: (0,) * len(shape))


STEPS = 4
NEAR = ((0, 0), (1, 0), (2, 0), (3, 0), (0, 1))
FAR = ((1, 1), (2, 1), (3, 1))


def partial_call(pieces, keys, weights, out_shape, out_specs, finish_step):
    w0, w1 = weights
    depth, width = w0.shape
    block = width // STEPS
    flat = [pieces[k] for k in keys]
    count = len(flat)
    rows = flat[0].shape[0]
    total = count * rows

    def body(*refs):
        w0_ref, w1_ref = refs[count : count + 2]
        outs, left, acc = refs[count + 2 : -2], refs[-2], refs[-1]
        j = pl.program_id(0)

        @pl.when(j == 0)
        def _():
            for n in range(count):
                left[n * rows : (n + 1) * rows] = refs[n][...]

        right = jnp.concatenate([w0_ref[...], w1_ref[...]], axis=0)
        value = jnp.dot(left[...], right, preferred_element_type=F32)
        finish_step(j, value, outs, acc)

    return pl.pallas_call(
        body,
        grid=(STEPS,),
        in_specs=[full(v.shape) for v in flat]
        + [pl.BlockSpec((depth, block), lambda j: (0, j))] * 2,
        out_specs=out_specs,
        out_shape=out_shape,
        scratch_shapes=[
            pltpu.VMEM((total, 2 * depth), BF16),
            pltpu.VMEM((STEPS, total, block), F32),
        ],
    )(*flat, w0, w1)


def sends(pieces, weights, rows, width):
    a = ROWS_SUM
    shapes = [(3, a, width + LANES)] + [(rows - a, width + LANES)] * 3

    def step(j, value, outs, acc):
        acc[j] = value

        @pl.when(j == STEPS - 1)
        def _():
            for k in range(3):
                whole = jnp.concatenate(
                    [acc[s, k * rows : (k + 1) * rows] for s in range(STEPS)], axis=1
                )
                put(outs[0], (k, slice(None)), whole[:a])
                put(outs[1 + k], (slice(None),), whole[a:])

    return partial_call(
        pieces, FAR, weights,
        [jax.ShapeDtypeStruct(s, jnp.int16) for s in shapes],
        [full(s) for s in shapes], step,
    )


def keeps(pieces, keys, weights, width):
    total = len(keys) * pieces[keys[0]].shape[0]

    def step(j, value, outs, acc):
        outs[0][...] = value

    return partial_call(
        pieces, keys, weights,
        jax.ShapeDtypeStruct((total, width), F32),
        pl.BlockSpec((total, width // STEPS), lambda j: (0, j)), step,
    )


def combine_y(kept, received, rows, width):
    a = ROWS_SUM

    def body(kept_ref, got, o1, o2, o3):
        k = pl.program_id(0)
        first = kept_ref[:a] + get(got, (0, slice(None)))
        for i, out in enumerate((o1, o2, o3)):

            @pl.when(k == i)
            def _(out=out):
                put(out, (slice(0, a),), first)
                put(out, (slice(a, rows),), kept_ref[a:])

    shape = (rows, width + LANES)
    return pl.pallas_call(
        body,
        grid=(3,),
        in_specs=[
            pl.BlockSpec((rows, width), lambda k: (k, 0)),
            pl.BlockSpec((1, a, width + LANES), lambda k: (k, 0, 0)),
        ],
        out_specs=[full(shape)] * 3,
        out_shape=[jax.ShapeDtypeStruct(shape, jnp.int16)] * 3,
        name="combine_y",
    )(kept, received)


def combine_x(kept, received, rows, width):
    a = ROWS_SUM

    def body(kept_ref, g1, g2, g3, out, token):
        last = kept_ref[a:] + get(g1, (slice(None),)) + get(g2, (slice(None),)) + get(g3, (slice(None),))
        put(out, (slice(0, a),), kept_ref[:a])
        put(out, (slice(a, rows),), last)
        token[...] = jnp.zeros((8, LANES), jnp.int32)

    shape = (rows, width + LANES)
    return pl.pallas_call(
        body,
        grid=(1,),
        in_specs=[pl.BlockSpec((rows, width), lambda k: (0, 0))]
        + [full(received[0].shape)] * 3,
        out_specs=[full(shape), full((8, LANES))],
        out_shape=[
            jax.ShapeDtypeStruct(shape, jnp.int16),
            jax.ShapeDtypeStruct((8, LANES), jnp.int32),
        ],
        name="combine_x",
    )(kept, *received)


def upright(line):
    return jnp.transpose(jnp.broadcast_to(line, (LANES, LANES)))


def finish(kept, received, ids, place, rows, width):
    def body(place_ref, kept_ref, g1, g2, g3, g4, ids_ref, e_ref, stat_ref):
        logits = kept_ref[...]
        for g in (g1, g2, g3, g4):
            logits = logits + get(g, (slice(None),))
        columns = lax.broadcasted_iota(jnp.int32, (rows, width), 1) + place_ref[1]
        label = upright(ids_ref[pl.ds(place_ref[0], 1), :])
        hit = columns.astype(F32) == label[:, :1]
        peak = jnp.max(logits, axis=1, keepdims=True)
        raised = jnp.exp(logits - peak)
        total = jnp.sum(raised, axis=1, keepdims=True)
        picked = jnp.sum(jnp.where(hit, logits, 0.0), axis=1, keepdims=True)
        e_ref[...] = raised.astype(BF16)
        lines = [jnp.transpose(jnp.broadcast_to(v, (rows, LANES)))[:1] for v in (peak, total, picked)]
        lines = jnp.concatenate(lines + [jnp.zeros((5, rows), F32)], axis=0)
        for k in range(16):
            stat_ref[k] = lines

    return pl.pallas_call(
        body,
        grid=(1,),
        in_specs=[
            pl.BlockSpec(memory_space=pltpu.SMEM),
            pl.BlockSpec((rows, width), lambda k: (1, 0)),
        ]
        + [full(received[0].shape)] * 4
        + [full(ids.shape)],
        out_specs=[full((rows, width)), full((16, 8, rows))],
        out_shape=[
            jax.ShapeDtypeStruct((rows, width), BF16),
            jax.ShapeDtypeStruct((16, 8, rows), F32),
        ],
        name="finish",
    )(place, kept, *received, ids)


def settle(every, stats):
    def body(every_ref, own_ref, loss_ref, factor_ref):
        peaks, totals, picks = (every_ref[:, k] for k in range(3))
        top = jnp.max(peaks, axis=0, keepdims=True)
        total = jnp.sum(totals * jnp.exp(peaks - top), axis=0, keepdims=True)
        picked = jnp.sum(picks, axis=0, keepdims=True)
        loss_ref[...] = top + jnp.log(total) - picked
        factor = jnp.exp(own_ref[0, :1] - top) / total
        factor_ref[...] = jnp.broadcast_to(factor, factor_ref.shape)

    rows = every.shape[-1]
    return pl.pallas_call(
        body,
        out_shape=[
            jax.ShapeDtypeStruct((1, rows), F32),
            jax.ShapeDtypeStruct((8, rows), F32),
        ],
        name="settle",
    )(every, stats)


def slopes(pieces, spans, factors, ids, place, width):
    sizes = [p.shape[0] for p in pieces]
    total = sum(sizes)

    def body(place_ref, *refs):
        ins, factor_refs, ids_ref, out = refs[:-6], refs[-6:-2], refs[-2], refs[-1]
        columns = lax.broadcasted_iota(jnp.int32, (max(sizes), width), 1) + place_ref[1]
        columns = columns.astype(F32)
        at = 0
        for ref, n, (k, a, b) in zip(ins, sizes, spans):
            owner = place_ref[2 + k]
            dy, dx = (NEAR + FAR)[k]
            scale = upright(factor_refs[dy][dx, :1])[a:b, :1]
            label = upright(ids_ref[pl.ds(owner, 1), :])[a:b, :1]
            value = ref[...].astype(F32) * scale
            value = value - jnp.where(columns[:n] == label, 1.0, 0.0)
            out[at : at + n] = value.astype(BF16)
            at += n

    return pl.pallas_call(
        body,
        grid=(1,),
        in_specs=[pl.BlockSpec(memory_space=pltpu.SMEM)]
        + [full(p.shape) for p in pieces]
        + [full(f.shape) for f in factors]
        + [full(ids.shape)],
        out_specs=full((total, width)),
        out_shape=jax.ShapeDtypeStruct((total, width), BF16),
    )(place, *pieces, *factors, ids)


def turned(token, pieces, rows, depth):
    g = ROWS_OUT
    flat = [pieces[k] for k in NEAR + FAR]

    def body(token_ref, *refs):
        ins, (mine, theirs) = refs[:8], refs[8:]
        far = [r[...] for r in ins[5:]]
        far = jnp.concatenate([f[:g] for f in far] + [f[g:] for f in far], axis=0)
        parts = [r[...] for r in ins[:5]] + [far[k * rows : (k + 1) * rows] for k in range(3)]
        for k, part in enumerate(parts):
            flipped = jnp.transpose(part)
            mine[:, k * rows : (k + 1) * rows] = flipped[:depth]
            theirs[:, k * rows : (k + 1) * rows] = flipped[depth:]

    shape = (depth, 8 * rows)
    return pl.pallas_call(
        body,
        grid=(1,),
        in_specs=[full(token.shape)] + [full(v.shape) for v in flat],
        out_specs=[full(shape)] * 2,
        out_shape=[jax.ShapeDtypeStruct(shape, BF16)] * 2,
        name="turned",
    )(token, *flat)


def gradient(mine, theirs, near, near_other, far, far_other):
    depth = mine.shape[0]
    n, width = near.shape
    m = far.shape[0]
    block = width // STEPS

    def body(m_ref, t_ref, a_ref, b_ref, c_ref, d_ref, out):
        left = jnp.concatenate([m_ref[...], t_ref[...]], axis=1)
        right = jnp.concatenate([a_ref[...], c_ref[...], b_ref[...], d_ref[...]], axis=0)
        out[...] = jnp.dot(left, right, preferred_element_type=F32)

    col = lambda r: pl.BlockSpec((r, block), lambda j: (0, j))
    return pl.pallas_call(
        body,
        grid=(STEPS,),
        in_specs=[full(mine.shape)] * 2 + [col(n)] * 2 + [col(m)] * 2,
        out_specs=col(depth),
        out_shape=jax.ShapeDtypeStruct((depth, width), F32),
        name="gradient",
    )(mine, theirs, near, near_other, far, far_other)


def per_device(hidden, head_weight, targets):
    here = lax.axis_index("dp")
    block_index = lax.axis_index("vocab")
    c = here % C
    x = (here // C) % X
    y = here // (C * X)
    rows = hidden.shape[0]
    depth, width = head_weight.shape

    def columns_for(dy, dx):
        chip = ((y - dy) % Y) * X + (x ^ dx)
        own = lax.dynamic_slice_in_dim(hidden, (chip * C + c) * depth, depth, 1)
        other = lax.dynamic_slice_in_dim(hidden, (chip * C + 1 - c) * depth, depth, 1)
        return jnp.concatenate([own, other], axis=1)

    def outside(dy):
        return lambda y, x, c, h, z: (y + dy, x ^ 1, c, h ^ 1, z)

    weights = (head_weight, from_core(head_weight))
    pieces = {
        (2, 1): fetch(columns_for(2, 1), lambda y, x, c, h, z: (y + 2, x ^ 1, c, h, z)),
        (1, 1): fetch(columns_for(1, 1), outside(1)),
        (3, 1): fetch(columns_for(3, 1), outside(3)),
        (2, 0): from_y(columns_for(2, 0), 2),
        (1, 0): from_y(columns_for(1, 0), 1),
        (3, 0): from_y(columns_for(3, 0), 3),
        (0, 1): from_x(columns_for(0, 1)),
        (0, 0): columns_for(0, 0),
    }

    to_x, *to_y = sends(pieces, weights, rows, width)
    got_x = from_x(to_x)
    got_y = [from_y(v, -dy) for v, dy in zip(to_y, (1, 2, 3))]
    kept_y = keeps(pieces, NEAR[1:4], weights, width)
    kept_x = keeps(pieces, (NEAR[4], NEAR[0]), weights, width)
    send_y = combine_y(kept_y, got_x, rows, width)
    send_x, token = combine_x(kept_x, got_y, rows, width)
    received = [from_x(send_x)]
    received += [from_y(v, -dy) for v, dy in zip(send_y, (1, 2, 3))]

    mine, sent = turned(token, pieces, rows, depth)
    token = token[0, 0]
    theirs = from_core(sent)
    ids = (targets + token).astype(F32).reshape(16, rows)
    owners = [(((y + dy) % Y) * X + (x ^ dx)) * C + c for dy, dx in NEAR + FAR]
    place = jnp.stack([here, block_index * width, *owners]).astype(jnp.int32)
    raised, stats = finish(kept_x, received, ids, place, rows, width)

    g = ROWS_OUT
    side_x = from_x(raised)
    along = {dy: from_y(raised, dy) for dy in (2, 1, 3)}
    far_y = {dy: from_y(side_x[g:], dy) for dy in (2, 1, 3)}
    far_x = {dy: from_x(along[dy][:g]) for dy in (1, 3, 2)}

    every = lax.all_to_all(stats, "vocab", 0, 0, tiled=True)
    loss, factor = settle(every, stats)
    pair = jnp.stack([factor, from_x(factor)])
    factors = [pair] + [from_y(pair, dy) for dy in (1, 2, 3)]

    near_spans = [(k, 0, rows) for k in range(5)]
    far_spans = [(5 + k, 0, g) for k in range(3)] + [(5 + k, g, rows) for k in range(3)]
    slope_near = slopes(
        [raised, along[1], along[2], along[3], side_x],
        near_spans, factors, ids, place, width,
    )
    slope_far = slopes(
        [far_x[d] for d in (1, 2, 3)] + [far_y[d] for d in (1, 2, 3)],
        far_spans, factors, ids, place, width,
    )
    near_other = from_core(slope_near)
    far_other = from_core(slope_far)
    grad = gradient(mine, theirs, slope_near, near_other, slope_far, far_other)
    return (loss.reshape(rows), grad)


def solution(mesh):
    in_specs = (P("dp", None), P("dp", "vocab"), P())
    out_specs = (P("dp"), P("dp", "vocab"))

    return jax.shard_map(
        per_device, mesh=mesh, in_specs=in_specs, out_specs=out_specs, check_vma=False
    )
```
